32 devices in a mesh: fsdp: 4 (over x, core), tp: 8 (over z, y).
Axes of the slice: x: 2, y: 2, z: 4, core: 2. Of those that a mesh axis runs over, the one named last changes fastest.
Arguments:
- hidden_in: bfloat16 [8, 1024, 1024], P('fsdp', 'tp'), may hold values from -6 to 6
- grad_out: bfloat16 [8, 1024, 1024], P('fsdp', 'tp'), may hold values from -6 to 6
- condition: float32 [8, 1024], P('fsdp', 'tp'), may hold values from -6 to 6
- w_mod: bfloat16 [1024, 6144], P('tp', 'fsdp'), may hold values from -0.1875 to 0.1875
- b_mod: bfloat16 [6144], P('fsdp'), may hold values from -3 to 3
- w_qkv: bfloat16 [1024, 16, 192], P('fsdp', 'tp'), may hold values from -0.1875 to 0.1875
- b_qv: bfloat16 [16, 128], P('tp', 'fsdp'), may hold values from -2 to 2
- w_proj: bfloat16 [1024, 1024], P('tp', 'fsdp'), may hold values from -2 to 2
- b_proj: bfloat16 [1024], P('fsdp'), may hold values from -3 to 3
- w_fc1: bfloat16 [1024, 4096], P('fsdp', 'tp'), may hold values from -0.1875 to 0.1875
- b_fc1: bfloat16 [4096], P(('tp', 'fsdp')), may hold values from -3 to 3
- w_fc2: bfloat16 [4096, 1024], P('tp', 'fsdp'), may hold values from -0.375 to 0.375
- b_fc2: bfloat16 [1024], P('fsdp'), may hold values from -3 to 3
Outputs:
- block_out: float32 [8, 1024, 1024], P('fsdp', 'tp')
- grad_input: float32 [8, 1024, 1024], P('fsdp', 'tp')
- grad_cond: float32 [8, 1024], P('fsdp', 'tp')
- grad_w_mod: float32 [1024, 6144], P('tp', 'fsdp')
- grad_b_mod: float32 [6144], P('fsdp')
- grad_w_qkv: float32 [1024, 16, 192], P('fsdp', 'tp')
- grad_b_qv: float32 [16, 128], P('tp', 'fsdp')
- grad_w_proj: float32 [1024, 1024], P('tp', 'fsdp')
- grad_b_proj: float32 [1024], P('fsdp')
- grad_w_fc1: float32 [1024, 4096], P('fsdp', 'tp')
- grad_b_fc1: float32 [4096], P(('tp', 'fsdp'))
- grad_w_fc2: float32 [4096, 1024], P('tp', 'fsdp')
- grad_b_fc2: float32 [1024], P('fsdp')
The draws below stay inside these ranges and needn't reach their ends.
All inputs are finite; a program needn't handle non-finite values.
Results may differ from the reference program's by a relative error of at most 0.013.
The reference program's roundings to bfloat16 on the way count: a program that leaves them out, or rounds other values in their place, can miss the bound.
Values may be sent and summed in bfloat16 or wider, within the bound.
No kernel may reach another device: no remote copies, remote signals or barrier semaphores. Data moves between devices by JAX's collectives and lax.ppermute only.
A program may use at most 128 MiB of HBM per device.

```python
import jax
import jax.numpy as jnp
from jax import lax

D = 1024
H = 16
HD = 64
FF = 4096
C = 1024
S = 1024
LATENTS = 8


def draw_b_qv(key, part):
    base_key = jax.random.fold_in(key, 11)
    key_one = jax.random.fold_in(base_key, 0)
    values = jnp.clip(jax.random.normal(key_one, (H, 2 * HD), jnp.float32), -4.0, 4.0)
    return (values * 0.5).astype(jnp.bfloat16)


def block_levels(own_key, dims, cuts, smallest, high):
    gain, own = 1.0, jax.random.fold_in(own_key, 6)
    for position, shards_of in cuts:
        steps = jnp.exp(jax.random.uniform(jax.random.fold_in(own, position), (shards_of,), jnp.float32, smallest / len(cuts), high / len(cuts)))
        gain = gain * jnp.repeat(steps, dims[position] // shards_of).reshape([-1 if axis == position else 1 for axis in range(len(dims))])
    return gain


def noise(rng, shape, width, limit, cuts=(), kind=jnp.bfloat16):
    values = jax.random.normal(rng, shape, jnp.float32) * width
    if len(cuts) > 0:
        values = block_levels(rng, shape, cuts, -0.22, 0.18) * values
    return jnp.clip(values, min=-limit, max=limit).astype(kind)


def setup_inputs(seed: int = 0) -> dict:
    streams_of = jax.random.split(jax.random.key(seed), 14)
    hidden_in = noise(streams_of[0], (LATENTS, S, D), 1.0, 6.0, ((0, 4), (1, 8)))
    grad_out = noise(streams_of[1], (LATENTS, S, D), 1.0, 6.0, ((0, 4), (1, 8)))
    condition = noise(streams_of[2], (LATENTS, C), 1.0, 6.0, ((0, 4), (1, 8)), jnp.float32)
    w_mod = noise(streams_of[3], (C, 6 * D), C ** -0.5, 0.1875, ((0, 8), (1, 4)))
    b_mod = noise(streams_of[4], (6 * D,), 0.5, 3.0, ((0, 4),))
    w_qkv = noise(streams_of[5], (D, H, 3 * HD), D ** -0.5, 0.1875, ((0, 4), (1, 8)))
    b_qv = draw_b_qv(jax.random.fold_in(streams_of[13], 71), 0)
    w_proj = noise(streams_of[7], (D, D), (max(HD // 8, 1)) ** -0.5, 2.0, ((0, 8), (1, 4)))
    b_proj = noise(streams_of[8], (D,), 0.5, 3.0, ((0, 4),))
    w_fc1 = noise(streams_of[9], (D, FF), D ** -0.5, 0.1875, ((0, 4), (1, 8)))
    b_fc1 = noise(streams_of[10], (FF,), 0.5, 3.0, ((0, 32),))
    w_fc2 = noise(streams_of[11], (FF, D), (FF // 16) ** -0.5, 0.375, ((0, 8), (1, 4)))
    b_fc2 = noise(streams_of[12], (D,), 0.5, 3.0, ((0, 4),))
    return dict(hidden_in=hidden_in, grad_out=grad_out, condition=condition, w_mod=w_mod, b_mod=b_mod, w_qkv=w_qkv, b_qv=b_qv, w_proj=w_proj, b_proj=b_proj, w_fc1=w_fc1, b_fc1=b_fc1, w_fc2=w_fc2, b_fc2=b_fc2)


EPSILON = 1e-06

def layer_norm(values):
    center_mean = lax.optimization_barrier(jnp.mean(values, -1, keepdims=True))
    centered = values - center_mean
    variance = lax.optimization_barrier(jnp.mean(centered * centered, -1, keepdims=True))
    inv_std = lax.rsqrt(variance + EPSILON)
    return (centered * inv_std, inv_std)

def norm_back(grad_normed, normed, inv_std):
    return inv_std * (grad_normed - lax.optimization_barrier(jnp.mean(grad_normed, -1, keepdims=True)) - normed * lax.optimization_barrier(jnp.mean(grad_normed * normed, -1, keepdims=True)))

def gelu_tanh(values):
    return jax.nn.gelu(values, approximate=True)

def attend_one(query_rows, key_rows, value_rows):
    score_scale = query_rows.shape[-1] ** (-0.5)
    scores = jnp.einsum('qhe,khe->hqk', query_rows.astype(jnp.float32), key_rows.astype(jnp.float32)) * score_scale
    row_max = lax.optimization_barrier(jnp.max(scores, -1, keepdims=True))
    log_total = row_max + jnp.log(lax.optimization_barrier(jnp.sum(jnp.exp(scores - row_max), -1, keepdims=True)))
    probs_low = jnp.exp(scores - log_total).astype(jnp.bfloat16)
    attended = jnp.einsum('hqk,khe->qhe', probs_low.astype(jnp.float32), value_rows.astype(jnp.float32))
    return (attended.astype(jnp.bfloat16), log_total)

def attend_back(query_rows, key_rows, value_rows, log_total, grad_attended):
    score_scale = query_rows.shape[-1] ** (-0.5)
    query_f = query_rows.astype(jnp.float32)
    key_f = key_rows.astype(jnp.float32)
    grad_f = grad_attended.astype(jnp.float32)
    scores = jnp.einsum('qhe,khe->hqk', query_f, key_f) * score_scale
    probs = jnp.exp(scores - log_total)
    probs_low = probs.astype(jnp.bfloat16)
    grad_probs = jnp.einsum('qhe,khe->hqk', grad_f, value_rows.astype(jnp.float32))
    inner = lax.optimization_barrier(jnp.sum(probs * grad_probs, -1, keepdims=True))
    grad_scores = (probs * (grad_probs - inner)).astype(jnp.bfloat16).astype(jnp.float32)
    grad_query = jnp.einsum('hqk,khe->qhe', grad_scores, key_f) * score_scale
    grad_keys = jnp.einsum('hqk,qhe->khe', grad_scores, query_f) * score_scale
    grad_values = jnp.einsum('hqk,qhe->khe', probs_low.astype(jnp.float32), grad_f)
    return jnp.concatenate([grad_query, grad_keys, grad_values], -1).astype(jnp.bfloat16)

def reference(hidden_in, grad_out, condition, w_mod, b_mod, w_qkv, b_qv, w_proj, b_proj, w_fc1, b_fc1, w_fc2, b_fc2):
    qkv_matrix = w_qkv.reshape(D, H * 3 * HD)
    qv_float = b_qv.astype(jnp.float32)
    bias_three = jnp.concatenate([qv_float[:, :HD], jnp.zeros((H, HD), jnp.float32), qv_float[:, HD:]], -1)

    def one_latent(totals, items):
        tokens, cot_low, cond_row = items
        cond_act, silu_back = jax.vjp(jax.nn.silu, cond_row)
        cond_low = cond_act.astype(jnp.bfloat16)
        modulation = jnp.dot(cond_low[None, :], w_mod, preferred_element_type=jnp.float32)[0] + b_mod.astype(jnp.float32)
        shift_one = modulation[0:D]
        scale_one = modulation[D:2 * D]
        gate_one = modulation[2 * D:3 * D]
        shift_two = modulation[3 * D:4 * D]
        scale_two = modulation[4 * D:5 * D]
        gate_two = modulation[5 * D:6 * D]
        resid_in = tokens.astype(jnp.float32)
        normed_one, inv_one = layer_norm(resid_in)
        attn_in = (normed_one * (1.0 + scale_one) + shift_one).astype(jnp.bfloat16)
        projected = (jnp.dot(attn_in, qkv_matrix, preferred_element_type=jnp.float32).reshape(S, H, 3 * HD) + bias_three).astype(jnp.bfloat16)
        query_rows = projected[..., :HD]
        key_rows = projected[..., HD:2 * HD]
        value_rows = projected[..., 2 * HD:]
        attended, log_total = attend_one(query_rows, key_rows, value_rows)
        attended_flat = attended.reshape(S, D)
        attn_branch = jnp.dot(attended_flat, w_proj, preferred_element_type=jnp.float32) + b_proj.astype(jnp.float32)
        resid_mid = resid_in + gate_one * attn_branch
        normed_two, inv_two = layer_norm(resid_mid)
        mlp_in = (normed_two * (1.0 + scale_two) + shift_two).astype(jnp.bfloat16)
        pre_act = jnp.dot(mlp_in, w_fc1, preferred_element_type=jnp.float32) + b_fc1.astype(jnp.float32)
        act_float, gelu_back = jax.vjp(gelu_tanh, pre_act)
        act_low = act_float.astype(jnp.bfloat16)
        mlp_branch = jnp.dot(act_low, w_fc2, preferred_element_type=jnp.float32) + b_fc2.astype(jnp.float32)
        block_out = resid_mid + gate_two * mlp_branch
        cotangent = cot_low.astype(jnp.float32)
        grad_gate_two = lax.optimization_barrier(jnp.sum(cotangent * mlp_branch, 0))
        grad_mlp_out = (gate_two * cotangent).astype(jnp.bfloat16)
        grad_fc2 = jnp.dot(act_low.T, grad_mlp_out, preferred_element_type=jnp.float32)
        grad_fc2_bias = lax.optimization_barrier(jnp.sum(grad_mlp_out.astype(jnp.float32), 0))
        grad_act = jnp.dot(grad_mlp_out, w_fc2.T, preferred_element_type=jnp.float32)
        grad_pre = gelu_back(grad_act)[0].astype(jnp.bfloat16)
        grad_fc1 = jnp.dot(mlp_in.T, grad_pre, preferred_element_type=jnp.float32)
        grad_fc1_bias = lax.optimization_barrier(jnp.sum(grad_pre.astype(jnp.float32), 0))
        grad_mlp_in = jnp.dot(grad_pre, w_fc1.T, preferred_element_type=jnp.float32)
        grad_scale_two = lax.optimization_barrier(jnp.sum(grad_mlp_in * normed_two, 0))
        grad_shift_two = lax.optimization_barrier(jnp.sum(grad_mlp_in, 0))
        grad_mid = cotangent + norm_back(grad_mlp_in * (1.0 + scale_two), normed_two, inv_two)
        grad_gate_one = lax.optimization_barrier(jnp.sum(grad_mid * attn_branch, 0))
        grad_attn_out = (gate_one * grad_mid).astype(jnp.bfloat16)
        grad_proj = jnp.dot(attended_flat.T, grad_attn_out, preferred_element_type=jnp.float32)
        grad_proj_bias = lax.optimization_barrier(jnp.sum(grad_attn_out.astype(jnp.float32), 0))
        grad_attended = jnp.dot(grad_attn_out, w_proj.T, preferred_element_type=jnp.float32).astype(jnp.bfloat16)
        grad_projected = attend_back(query_rows, key_rows, value_rows, log_total, grad_attended.reshape(S, H, HD))
        grad_flat = grad_projected.reshape(S, H * 3 * HD)
        grad_qkv = jnp.dot(attn_in.T, grad_flat, preferred_element_type=jnp.float32).reshape(D, H, 3 * HD)
        bias_sums = lax.optimization_barrier(jnp.sum(grad_projected.astype(jnp.float32), 0))
        grad_qv_bias = jnp.concatenate([bias_sums[:, :HD], bias_sums[:, 2 * HD:]], -1)
        grad_attn_in = jnp.dot(grad_flat, qkv_matrix.T, preferred_element_type=jnp.float32)
        grad_scale_one = lax.optimization_barrier(jnp.sum(grad_attn_in * normed_one, 0))
        grad_shift_one = lax.optimization_barrier(jnp.sum(grad_attn_in, 0))
        grad_input = grad_mid + norm_back(grad_attn_in * (1.0 + scale_one), normed_one, inv_one)
        grad_modulation = jnp.concatenate([grad_shift_one, grad_scale_one, grad_gate_one, grad_shift_two, grad_scale_two, grad_gate_two], -1)
        grad_mod_low = grad_modulation.astype(jnp.bfloat16)
        grad_mod_w = jnp.dot(cond_low[:, None], grad_mod_low[None, :], preferred_element_type=jnp.float32)
        grad_cond = silu_back(jnp.dot(grad_mod_low[None, :], w_mod.T, preferred_element_type=jnp.float32)[0])[0]
        terms = (grad_mod_w, grad_modulation, grad_qkv, grad_qv_bias, grad_proj, grad_proj_bias, grad_fc1, grad_fc1_bias, grad_fc2, grad_fc2_bias)
        new_totals = tuple((total + term for total, term in zip(totals, terms)))
        return (new_totals, (block_out, grad_input, grad_cond))
    start = (jnp.zeros((C, 6 * D), jnp.float32), jnp.zeros((6 * D,), jnp.float32), jnp.zeros((D, H, 3 * HD), jnp.float32), jnp.zeros((H, 2 * HD), jnp.float32), jnp.zeros((D, D), jnp.float32), jnp.zeros((D,), jnp.float32), jnp.zeros((D, FF), jnp.float32), jnp.zeros((FF,), jnp.float32), jnp.zeros((FF, D), jnp.float32), jnp.zeros((D,), jnp.float32))
    totals, stacked = lax.scan(one_latent, start, (hidden_in, grad_out, condition))
    return (stacked[0], stacked[1], stacked[2], totals[0], totals[1], totals[2], totals[3], totals[4], totals[5], totals[6], totals[7], totals[8], totals[9])
```

```python
import jax
import jax.numpy as jnp
from jax import lax
from jax.sharding import Mesh
from jax.sharding import PartitionSpec as P

EPSILON = 1e-06
LOW = jnp.bfloat16
F32 = jnp.float32


def layer_norm(values):
    center_mean = jnp.mean(values, -1, keepdims=True)
    centered = values - center_mean
    variance = jnp.mean(centered * centered, -1, keepdims=True)
    inv_std = lax.rsqrt(variance + EPSILON)
    return (centered * inv_std, inv_std)


def norm_back(grad_normed, normed, inv_std):
    return inv_std * (
        grad_normed
        - jnp.mean(grad_normed, -1, keepdims=True)
        - normed * jnp.mean(grad_normed * normed, -1, keepdims=True)
    )


def gelu_tanh(values):
    return jax.nn.gelu(values, approximate=True)


def dot(left, right):
    return jnp.dot(left, right, preferred_element_type=F32)


def attend_one(query_rows, key_rows, value_rows):
    score_scale = query_rows.shape[-1] ** (-0.5)
    scores = (
        jnp.einsum("qhe,khe->hqk", query_rows, key_rows, preferred_element_type=F32) * score_scale
    )
    row_max = jnp.max(scores, -1, keepdims=True)
    log_total = row_max + jnp.log(jnp.sum(jnp.exp(scores - row_max), -1, keepdims=True))
    probs_low = jnp.exp(scores - log_total).astype(LOW)
    attended = jnp.einsum("hqk,khe->qhe", probs_low, value_rows, preferred_element_type=F32)
    return (attended.astype(LOW), log_total)


def attend_back(query_rows, key_rows, value_rows, log_total, grad_attended):
    score_scale = query_rows.shape[-1] ** (-0.5)
    scores = (
        jnp.einsum("qhe,khe->hqk", query_rows, key_rows, preferred_element_type=F32) * score_scale
    )
    probs = jnp.exp(scores - log_total)
    probs_low = probs.astype(LOW)
    grad_probs = jnp.einsum("qhe,khe->hqk", grad_attended, value_rows, preferred_element_type=F32)
    inner = jnp.sum(probs * grad_probs, -1, keepdims=True)
    grad_scores = (probs * (grad_probs - inner)).astype(LOW)
    grad_query = (
        jnp.einsum("hqk,khe->qhe", grad_scores, key_rows, preferred_element_type=F32) * score_scale
    )
    grad_keys = (
        jnp.einsum("hqk,qhe->khe", grad_scores, query_rows, preferred_element_type=F32)
        * score_scale
    )
    grad_values = jnp.einsum("hqk,qhe->khe", probs_low, grad_attended, preferred_element_type=F32)
    return jnp.concatenate([grad_query, grad_keys, grad_values], -1).astype(LOW)


def relative(values, axis, place, count):
    twice = jnp.concatenate([values, values], axis)
    return lax.dynamic_slice_in_dim(twice, place, count, axis)


def absolute(values, axis, place, count):
    return relative(values, axis, (count - place) % count, count)


def from_offset(values, name, offset, count):
    return lax.ppermute(values, name, [((d + offset) % count, d) for d in range(count)])


def to_offset(values, name, offset, count):
    return lax.ppermute(values, name, [(d, (d + offset) % count) for d in range(count)])


def gather_rel(values, name, count):
    return [values] + [from_offset(values, name, o, count) for o in range(1, count)]


def scatter_rel(blocks, name, count):
    total = blocks[0].astype(F32)
    for o in range(1, count):
        total = total + to_offset(blocks[o].astype(LOW), name, o, count).astype(F32)
    return total


def pair_perm(offsets, counts):
    (o1, o2), (n1, n2) = offsets, counts
    return [
        (a * n2 + b, ((a + o1) % n1) * n2 + (b + o2) % n2) for a in range(n1) for b in range(n2)
    ]


def make_body(n_x, n_z, n_y):
    def on_device(
        hidden_in, grad_out, condition, w_mod, b_mod, w_qkv, b_qv, w_proj, b_proj, w_fc1, b_fc1,
        w_fc2, b_fc2,
    ):
        at_x, at_c = lax.axis_index("fx"), lax.axis_index("core")
        at_z, at_y = lax.axis_index("z"), lax.axis_index("y")
        held, piece, width = hidden_in.shape
        part = width // n_x
        heads_here = w_qkv.shape[1]
        head_dim = w_qkv.shape[2] // 3
        d_rows = w_qkv.shape[0]
        split_heads = heads_here % 2 == 0

        def swap_core(values):
            return lax.ppermute(values, "core", [(0, 1), (1, 0)])

        def by_core(own, other, axis=0):
            stacked = jnp.stack([own, other], axis)
            return jnp.where(at_c == 0, stacked, jnp.flip(stacked, axis))

        def pick(values, index, axis=0):
            return lax.dynamic_index_in_dim(values, index, axis, keepdims=False)

        at_s = at_z % held

        def route(step):
            pairs = []
            for core in range(2):
                for z_from in range(n_z):
                    latent = (z_from % held + step) % held
                    pairs.append(
                        (core * n_z + z_from, (z_from // held) * n_z + core * held + latent)
                    )
            return pairs

        def tokens_in(values):
            values = relative(
                values.reshape(held, piece, n_x, part), 2, at_x, n_x
            ).reshape(held, piece, width)
            got = [
                lax.ppermute(pick(values, (at_s + k) % held), ("core", "z"), route(k))
                for k in range(held)
            ]
            return jnp.concatenate(got, 0)

        def tokens_out(values):
            rows = values.astype(LOW).reshape(held, piece, width)
            got = [
                lax.ppermute(rows[k], ("core", "z"), [(d, s) for s, d in route(k)])
                for k in range(held)
            ]
            back = absolute(jnp.stack(got), 0, at_s, held)
            return absolute(
                back.reshape(held, piece, n_x, part), 2, at_x, n_x
            ).reshape(held, piece, width).astype(F32)

        def gather_tokens(own):
            over_y = gather_rel(own, "y", n_y)
            rows = []
            for values in over_y:
                rows += [values, swap_core(values)]
            return jnp.concatenate(rows, 0)

        def scatter_tokens(terms):
            blocks = terms.reshape(n_y, 2, terms.shape[0] // (2 * n_y), width)
            sums = [None] * n_y
            for r in list(range(1, n_y)) + [0]:
                sums[r] = blocks[r, 0] + swap_core(blocks[r, 1].astype(LOW)).astype(F32)
            return scatter_rel(sums, "y", n_y)

        hidden_own = tokens_in(hidden_in)
        hidden_full = gather_tokens(hidden_own)

        cond_act, silu_back = jax.vjp(jax.nn.silu, condition)
        cond_low = cond_act.astype(LOW)
        cond_pair = by_core(cond_low, swap_core(cond_low)).reshape(n_z, cond_low.shape[1])
        cond_all = relative(jnp.stack(gather_rel(cond_pair, "fx", n_x)), 1, at_z, n_z)
        features = cond_low.shape[1]
        cols = w_mod.shape[1]
        mod_terms = dot(cond_all.reshape(n_x * n_z, features), w_mod).reshape(n_x, n_z, cols)
        counts = (n_x, n_z)
        bias_here = jnp.where((at_z == 0) & (at_y == 0), b_mod.astype(F32), 0.0)
        mod_terms = mod_terms + bias_here
        mod_cols = [None] * n_x
        for ox in range(n_x):
            for oz in range(n_z):
                term = mod_terms[ox, oz]
                if ox or oz:
                    term = lax.ppermute(term, ("fx", "z"), pair_perm((ox, oz), counts))
                src = (-ox) % n_x
                mod_cols[src] = term if mod_cols[src] is None else mod_cols[src] + term
        mod_mine = jnp.stack(mod_cols)
        pair_counts = (2, n_y)
        own_sum, other_sum = mod_mine, None
        for oc in range(2):
            for oy in range(n_y):
                if oc == 0 and oy == 0:
                    continue
                got = lax.ppermute(mod_mine, ("core", "y"), pair_perm((oc, oy), pair_counts))
                if oc == 0:
                    own_sum = own_sum + got
                else:
                    other_sum = got if other_sum is None else other_sum + got
        modulation = by_core(own_sum, other_sum, 1)
        modulation = absolute(modulation, 0, at_x, n_x).reshape(6, n_x, part)
        modulation = relative(modulation, 1, at_x, n_x).reshape(6, 1, width)
        shift_one, scale_one, gate_one, shift_two, scale_two, gate_two = (
            modulation[i] for i in range(6)
        )

        def weight_in(halves, d_axis):
            own = pick(halves, at_c)
            got = swap_core(pick(halves, 1 - at_c))
            both = jnp.concatenate([own, got], d_axis)
            turned = jnp.concatenate([got, own], d_axis)
            both = jnp.where(at_c == 0, both, turned)
            over_z = jnp.concatenate(gather_rel(both, "z", n_z), 1 - d_axis)
            return jnp.concatenate(gather_rel(over_z, "fx", n_x), d_axis)

        def weight_whole(values, d_axis):
            got = swap_core(values)
            both = jnp.concatenate([values, got], d_axis)
            turned = jnp.concatenate([got, values], d_axis)
            both = jnp.where(at_c == 0, both, turned)
            over_z = absolute(jnp.stack(gather_rel(both, "z", n_z)), 0, at_z, n_z)
            mine = lax.dynamic_slice_in_dim(over_z, at_c * (n_z // 2), n_z // 2, 0)
            joined = jnp.concatenate([mine[i] for i in range(n_z // 2)], 1 - d_axis)
            return jnp.concatenate(gather_rel(joined, "fx", n_x), d_axis)

        flat_qkv = w_qkv.reshape(d_rows, heads_here * 3 * head_dim)
        if split_heads:
            q_halves = jnp.stack(jnp.split(flat_qkv, 2, 1))
            qkv_matrix = weight_in(q_halves, 0)
            proj_rows = weight_in(jnp.stack(jnp.split(w_proj, 2, 0)), 1)
        else:
            qkv_matrix = weight_whole(flat_qkv, 0)
            proj_rows = weight_whole(w_proj, 1)
        fc1_cols = weight_in(jnp.stack(jnp.split(w_fc1, 2, 1)), 0)
        fc2_rows = weight_in(jnp.stack(jnp.split(w_fc2, 2, 0)), 1)

        n_qv, n_f1, n_d = b_qv.size, b_fc1.size, b_proj.size
        packed = jnp.concatenate([b_qv.reshape(-1), b_fc1, b_proj, b_fc2])
        over_c = by_core(packed, swap_core(packed))
        over_x = jnp.stack(gather_rel(over_c, "fx", n_x))
        proj_bias = over_x[:, :, n_qv + n_f1 : n_qv + n_f1 + n_d].reshape(1, width).astype(F32)
        fc2_bias = over_x[:, :, n_qv + n_f1 + n_d :].reshape(1, width).astype(F32)
        tp_part = absolute(over_x[:, :, : n_qv + n_f1], 0, at_x, n_x).reshape(
            2 * n_x, n_qv + n_f1
        )
        over_z = jnp.stack(gather_rel(tp_part, "z", n_z))
        qv_all = over_z[:, :, :n_qv].reshape(n_z, 2 * n_x, heads_here, n_qv // heads_here)
        qv_all = qv_all.transpose(0, 2, 1, 3).reshape(n_z, heads_here, 2 * head_dim)
        if split_heads:
            qv_here = pick(qv_all.reshape(n_z, 2, heads_here // 2, 2 * head_dim), at_c, 1)
        else:
            qv_here = lax.dynamic_slice_in_dim(
                absolute(qv_all, 0, at_z, n_z), at_c * (n_z // 2), n_z // 2, 0
            )
        heads = n_z * heads_here // 2
        qv_here = qv_here.reshape(heads, 2 * head_dim).astype(F32)
        bias_three = jnp.concatenate(
            [qv_here[:, :head_dim], jnp.zeros((heads, head_dim), F32), qv_here[:, head_dim:]], -1
        ).reshape(1, heads * 3 * head_dim)
        fc1_bias = pick(over_z[:, :, n_qv:].reshape(n_z, 2, n_x * n_f1), at_c, 1)
        fc1_bias = fc1_bias.reshape(1, n_z * n_x * n_f1).astype(F32)

        resid_in = hidden_own.astype(F32)
        normed_one, inv_one = layer_norm(resid_in)
        attn_in = (
            layer_norm(hidden_full.astype(F32))[0] * (1.0 + scale_one) + shift_one
        ).astype(LOW)
        rows = attn_in.shape[0]
        projected = (dot(attn_in, qkv_matrix) + bias_three).astype(LOW)
        projected = projected.reshape(rows, heads, 3 * head_dim)
        query_rows = projected[..., :head_dim]
        key_rows = projected[..., head_dim : 2 * head_dim]
        value_rows = projected[..., 2 * head_dim :]
        attended, log_total = attend_one(query_rows, key_rows, value_rows)
        attended = attended.reshape(rows, heads * head_dim)
        attn_branch = scatter_tokens(dot(attended, proj_rows)) + proj_bias
        resid_mid = resid_in + gate_one * attn_branch
        normed_two, inv_two = layer_norm(resid_mid)
        mlp_in = gather_tokens((normed_two * (1.0 + scale_two) + shift_two).astype(LOW))
        pre_act = dot(mlp_in, fc1_cols) + fc1_bias
        act_float, gelu_back = jax.vjp(gelu_tanh, pre_act)
        act_low = act_float.astype(LOW)
        mlp_branch = scatter_tokens(dot(act_low, fc2_rows)) + fc2_bias
        block_out = tokens_out(resid_mid + gate_two * mlp_branch)

        grad_own = tokens_in(grad_out)
        grad_full = gather_tokens(grad_own)
        cotangent = grad_own.astype(F32)
        grad_gate_two = jnp.sum(cotangent * mlp_branch, 0)
        grad_mlp_out = (gate_two * grad_full.astype(F32)).astype(LOW)
        grad_fc2 = dot(act_low.T, grad_mlp_out)
        grad_fc2_bias = jnp.sum(grad_mlp_out.astype(F32), 0)
        grad_act = dot(grad_mlp_out, fc2_rows.T)
        grad_pre = gelu_back(grad_act)[0].astype(LOW)
        grad_fc1 = dot(mlp_in.T, grad_pre)
        grad_fc1_bias = jnp.sum(grad_pre.astype(F32), 0)
        grad_mlp_in = scatter_tokens(dot(grad_pre, fc1_cols.T))
        grad_scale_two = jnp.sum(grad_mlp_in * normed_two, 0)
        grad_shift_two = jnp.sum(grad_mlp_in, 0)
        grad_mid = cotangent + norm_back(grad_mlp_in * (1.0 + scale_two), normed_two, inv_two)
        grad_gate_one = jnp.sum(grad_mid * attn_branch, 0)
        grad_attn_out = gather_tokens((gate_one * grad_mid).astype(LOW))
        grad_proj = dot(attended.T, grad_attn_out)
        grad_proj_bias = jnp.sum(grad_attn_out.astype(F32), 0)
        grad_attended = dot(grad_attn_out, proj_rows.T).astype(LOW)
        grad_projected = attend_back(
            query_rows,
            key_rows,
            value_rows,
            log_total,
            grad_attended.reshape(rows, heads, head_dim),
        )
        grad_flat = grad_projected.reshape(rows, heads * 3 * head_dim)
        grad_attn_in = scatter_tokens(dot(grad_flat, qkv_matrix.T))
        grad_qkv = dot(attn_in.T, grad_flat)
        bias_sums = jnp.sum(grad_projected.astype(F32), 0)
        grad_qv = jnp.concatenate([bias_sums[:, :head_dim], bias_sums[:, 2 * head_dim :]], -1)
        grad_scale_one = jnp.sum(grad_attn_in * normed_one, 0)
        grad_shift_one = jnp.sum(grad_attn_in, 0)
        grad_input = tokens_out(
            grad_mid + norm_back(grad_attn_in * (1.0 + scale_one), normed_one, inv_one)
        )

        def sum_x(values, d_axis):
            return scatter_rel(jnp.split(values, n_x, d_axis), "fx", n_x)

        def to_core(values, d_axis):
            halves = jnp.stack(jnp.split(values, 2, d_axis))
            return pick(halves, at_c), swap_core(pick(halves, 1 - at_c))

        def weight_out(values, d_axis):
            total = sum_x(values, d_axis)
            total = scatter_rel(jnp.split(total, n_z, 1 - d_axis), "z", n_z)
            own, got = to_core(total, d_axis)
            joined = jnp.concatenate([own, got], 1 - d_axis)
            turned = jnp.concatenate([got, own], 1 - d_axis)
            return jnp.where(at_c == 0, joined, turned)

        def whole_out(values, d_axis):
            total = sum_x(values, d_axis)
            blocks = jnp.stack(jnp.split(total, n_z // 2, 1 - d_axis))
            blocks = lax.dynamic_update_slice_in_dim(
                jnp.zeros((n_z,) + blocks.shape[1:], F32), blocks, at_c * (n_z // 2), 0
            )
            blocks = relative(blocks, 0, at_z, n_z)
            total = scatter_rel([blocks[o] for o in range(n_z)], "z", n_z)
            own, got = to_core(total, d_axis)
            return own + got

        grad_w_fc2 = weight_out(grad_fc2, 1)
        grad_w_fc1 = weight_out(grad_fc1, 0)
        out_heads = weight_out if split_heads else whole_out
        grad_w_proj = out_heads(grad_proj, 1)
        grad_w_qkv = out_heads(grad_qkv, 0).reshape(d_rows, heads_here, 3 * head_dim)

        if split_heads:
            qv_rows = absolute(
                grad_qv.reshape(n_z, 1, heads_here // 2, 2 * head_dim), 0, at_z, n_z
            )
        else:
            qv_rows = grad_qv.reshape(n_z // 2, 1, heads_here, 2 * head_dim)
        f1_rows = absolute(grad_fc1_bias.reshape(n_z, n_x * n_f1), 0, at_z, n_z)
        d_sums = absolute(
            jnp.stack([grad_proj_bias, grad_fc2_bias], 1).reshape(n_x, part, 2), 0, at_x, n_x
        )
        small = jnp.concatenate(
            [qv_rows.reshape(-1), f1_rows.reshape(-1), d_sums.reshape(-1)]
        )
        small = sum(gather_rel(small, "fx", n_x))
        small = sum(gather_rel(small, "z", n_z))
        both = by_core(small, swap_core(small))
        n_q = qv_rows.size
        qv_both = both[:, :n_q]
        if split_heads:
            qv_z = pick(qv_both.reshape(2, n_z, heads_here // 2, 2 * head_dim), at_z, 1)
        else:
            qv_z = pick(qv_both.reshape(n_z, heads_here, 2 * head_dim), at_z, 0)
        qv_z = qv_z.reshape(heads_here, 2 * n_x, n_qv // heads_here)
        grad_b_qv = pick(qv_z, 2 * at_x + at_c, 1)
        f1_z = pick(both[:, n_q : n_q + f1_rows.size].reshape(2, n_z, n_x * n_f1), at_z, 1)
        grad_b_fc1 = pick(f1_z.reshape(2 * n_x, n_f1), 2 * at_x + at_c)
        d_here = pick(small[n_q + f1_rows.size :].reshape(2 * n_x, n_d, 2), 2 * at_x + at_c)
        grad_b_proj, grad_b_fc2 = d_here[:, 0], d_here[:, 1]

        grad_mod = jnp.stack(
            [
                grad_shift_one, grad_scale_one, grad_gate_one,
                grad_shift_two, grad_scale_two, grad_gate_two,
            ]
        )
        grad_mod = absolute(grad_mod.reshape(6, n_x, part), 1, at_x, n_x).reshape(n_x, 2, cols)
        grad_mine = pick(grad_mod, at_c, 1)
        grad_other = pick(grad_mod, 1 - at_c, 1)
        total = grad_mine
        for oc in range(2):
            for oy in range(n_y):
                if oc == 0 and oy == 0:
                    continue
                sent = grad_mine if oc == 0 else grad_other
                total = total + lax.ppermute(
                    sent, ("core", "y"), pair_perm((oc, oy), pair_counts)
                )
        total = relative(total, 0, at_x, n_x)
        all_rows = [None] * (n_x * n_z)
        for ox in range(n_x):
            for oz in range(n_z):
                row = total[ox]
                if ox or oz:
                    row = lax.ppermute(row, ("fx", "z"), pair_perm((ox, oz), counts))
                all_rows[((-ox) % n_x) * n_z + (-oz) % n_z] = row
        grad_modulation = jnp.stack(all_rows)
        grad_b_mod = jnp.sum(grad_modulation, 0)
        grad_mod_low = grad_modulation.astype(LOW)
        grad_w_mod = dot(cond_all.reshape(n_x * n_z, features).T, grad_mod_low)
        cond_terms = dot(grad_mod_low, w_mod.T).reshape(n_x, n_z, features)
        cond_terms = absolute(cond_terms, 1, at_z, n_z).reshape(n_x, 2, held, features)
        cond_terms = relative(cond_terms, 1, at_c, 2)
        total = cond_terms[0, 0]
        for ox in range(n_x):
            for oc in range(2):
                if ox or oc:
                    total = total + lax.ppermute(
                        cond_terms[ox, oc], ("fx", "core"), pair_perm((ox, oc), (n_x, 2))
                    )
        grad_cond = silu_back(total)[0]

        return (
            block_out, grad_input, grad_cond, grad_w_mod, grad_b_mod, grad_w_qkv, grad_b_qv,
            grad_w_proj, grad_b_proj, grad_w_fc1, grad_b_fc1, grad_w_fc2, grad_b_fc2,
        )

    return on_device


def solution(mesh):
    n_f, n_t = mesh.shape["fsdp"], mesh.shape["tp"]
    n_z = 4
    n_x, n_y = n_f // 2, n_t // n_z
    fine = Mesh(mesh.devices.reshape(n_x, 2, n_z, n_y), ("fx", "core", "z", "y"))
    f, t = ("fx", "core"), ("z", "y")
    weights = (
        P(t, f), P(f), P(f, t, None), P(t, f), P(t, f), P(f), P(f, t), P(t + f), P(t, f), P(f),
    )
    placed = (P(f, t, None), P(f, t, None), P(f, t)) + weights
    return jax.shard_map(
        make_body(n_x, n_z, n_y), mesh=fine, in_specs=placed, out_specs=placed, check_vma=False
    )
```

```python
import functools

import jax
import jax.numpy as jnp
from jax import lax
from jax.experimental import pallas as pl
from jax.experimental.pallas import tpu as pltpu
from jax.sharding import Mesh
from jax.sharding import PartitionSpec as P

EPSILON = 1e-06
LOW = jnp.bfloat16
F32 = jnp.float32


def layer_norm(values):
    center_mean = jnp.mean(values, -1, keepdims=True)
    centered = values - center_mean
    variance = jnp.mean(centered * centered, -1, keepdims=True)
    inv_std = lax.rsqrt(variance + EPSILON)
    return (centered * inv_std, inv_std)


def norm_back(grad_normed, normed, inv_std):
    return inv_std * (
        grad_normed
        - jnp.mean(grad_normed, -1, keepdims=True)
        - normed * jnp.mean(grad_normed * normed, -1, keepdims=True)
    )


def gelu_tanh(values):
    return jax.nn.gelu(values, approximate=True)


NT = (((1,), (1,)), ((), ()))
TN = (((0,), (0,)), ((), ()))
NN = (((1,), (0,)), ((), ()))


def mxu(left, right, dims):
    return lax.dot_general(left, right, dims, preferred_element_type=F32)


def attend_kernel(head_dim, query_ref, key_ref, value_ref, out_ref, log_ref):
    scale = head_dim ** (-0.5)
    for h in range(query_ref.shape[1] // head_dim):
        cols = slice(h * head_dim, (h + 1) * head_dim)
        scores = mxu(key_ref[:, cols], query_ref[:, cols], NT) * scale
        top = jnp.max(scores, 0, keepdims=True)
        weights = jnp.exp(scores - top)
        total = jnp.sum(weights, 0, keepdims=True)
        log_ref[h : h + 1, :] = top + jnp.log(total)
        probs_low = (weights * (1.0 / total)).astype(LOW)
        out_ref[:, cols] = mxu(value_ref[:, cols], probs_low, TN).T.astype(LOW)


def attend_back_kernel(
    head_dim, query_ref, key_ref, value_ref, log_ref, grad_ref, out_q, out_k, out_v, sum_k, sum_v
):
    scale = head_dim ** (-0.5)
    step = pl.program_id(0)

    @pl.when(step == 0)
    def _():
        sum_k[...] = jnp.zeros(sum_k.shape, F32)
        sum_v[...] = jnp.zeros(sum_v.shape, F32)

    for h in range(query_ref.shape[1] // head_dim):
        cols = slice(h * head_dim, (h + 1) * head_dim)
        query, key = query_ref[:, cols], key_ref[:, cols]
        grad = grad_ref[:, cols]
        scores = mxu(key, query, NT) * scale
        probs = jnp.exp(scores - log_ref[h : h + 1, :])
        grad_probs = mxu(value_ref[:, cols], grad, NT)
        inner = jnp.sum(probs * grad_probs, 0, keepdims=True)
        grad_scores = (probs * (grad_probs - inner)).astype(LOW)
        sum_v[:, cols] += mxu(probs.astype(LOW), grad, NN)
        sum_k[:, cols] += mxu(grad_scores, query, NN)
        out_q[:, cols] = (mxu(key, grad_scores, TN).T * scale).astype(LOW)

    @pl.when(step == pl.num_programs(0) - 1)
    def _():
        out_k[...] = (sum_k[...] * scale).astype(LOW)
        out_v[...] = sum_v[...].astype(LOW)


def attend(projected, head_dim, block):
    rows, span = projected.shape[0], projected.shape[1] // 3
    log_rows = max(8, span // head_dim)
    return pl.pallas_call(
        functools.partial(attend_kernel, head_dim),
        grid=(rows // block,),
        in_specs=[
            pl.BlockSpec((block, span), lambda i: (i, 0)),
            pl.BlockSpec((rows, span), lambda i: (0, 1)),
            pl.BlockSpec((rows, span), lambda i: (0, 2)),
        ],
        out_specs=[
            pl.BlockSpec((block, span), lambda i: (i, 0)),
            pl.BlockSpec((log_rows, block), lambda i: (0, i)),
        ],
        out_shape=[
            jax.ShapeDtypeStruct((rows, span), LOW),
            jax.ShapeDtypeStruct((log_rows, rows), F32),
        ],
        name="attend",
    )(projected, projected, projected)


def attend_back(projected, log_total, grad_attended, head_dim, block):
    rows, span = grad_attended.shape
    log_rows = log_total.shape[0]
    whole = pl.BlockSpec((rows, span), lambda i: (0, 0))
    by_block = pl.BlockSpec((block, span), lambda i: (i, 0))
    return pl.pallas_call(
        functools.partial(attend_back_kernel, head_dim),
        grid=(rows // block,),
        in_specs=[
            by_block,
            pl.BlockSpec((rows, span), lambda i: (0, 1)),
            pl.BlockSpec((rows, span), lambda i: (0, 2)),
            pl.BlockSpec((log_rows, block), lambda i: (0, i)),
            by_block,
        ],
        out_specs=[by_block, whole, whole],
        out_shape=[jax.ShapeDtypeStruct((rows, span), LOW)] * 3,
        scratch_shapes=[pltpu.VMEM((rows, span), F32), pltpu.VMEM((rows, span), F32)],
        name="attend_back",
    )(projected, projected, projected, log_total, grad_attended)


def relative(blocks, place):
    count = len(blocks)
    if count == 2:
        first, second = blocks
        return [jnp.where(place == 0, first, second), jnp.where(place == 0, second, first)]
    stacked = jnp.stack(blocks)
    return [
        lax.dynamic_index_in_dim(stacked, (o + place) % count, 0, keepdims=False)
        for o in range(count)
    ]


def absolute(blocks, place):
    return relative(blocks, (len(blocks) - place) % len(blocks))


def from_offset(values, name, offset, count):
    return lax.ppermute(values, name, [((d + offset) % count, d) for d in range(count)])


def to_offset(values, name, offset, count):
    return lax.ppermute(values, name, [(d, (d + offset) % count) for d in range(count)])


def gather_rel(values, name, count):
    return [values] + [from_offset(values, name, o, count) for o in range(1, count)]


def scatter_rel(blocks, name, count):
    total = blocks[0].astype(F32)
    for o in range(1, count):
        total = total + to_offset(blocks[o].astype(LOW), name, o, count).astype(F32)
    return total


def pair_perm(offsets, counts):
    (o1, o2), (n1, n2) = offsets, counts
    return [
        (a * n2 + b, ((a + o1) % n1) * n2 + (b + o2) % n2) for a in range(n1) for b in range(n2)
    ]


def widen(values, size):
    return jnp.pad(values, [(0, 0)] * (values.ndim - 1) + [(0, size - values.shape[-1])])


def make_body(n_x, n_z, n_y):
    def on_device(
        hidden_in, grad_out, condition, w_mod, b_mod, w_qkv, b_qv, w_proj, b_proj, w_fc1, b_fc1,
        w_fc2, b_fc2,
    ):
        at_x, at_c = lax.axis_index("fx"), lax.axis_index("core")
        at_z, at_y = lax.axis_index("z"), lax.axis_index("y")
        held, piece, width = hidden_in.shape
        assert n_z == 2 * held
        own_d, heads_here, three = w_qkv.shape
        head_dim = three // 3
        halved = heads_here % 2 == 0
        k_heads = heads_here // 2 if halved else heads_here
        z_mine = n_z if halved else n_z // 2
        heads = z_mine * k_heads

        def swap_core(values):
            return lax.ppermute(values, "core", [(0, 1), (1, 0)])

        def pick(values, index, axis=0):
            return lax.dynamic_index_in_dim(values, index, axis, keepdims=False)

        at_s = at_z % held

        def route(step):
            pairs = []
            for core in range(2):
                for z_from in range(n_z):
                    latent = (z_from % held + step) % held
                    pairs.append(
                        (core * n_z + z_from, (z_from // held) * n_z + core * held + latent)
                    )
            return pairs

        def tokens_in(values):
            rel = relative([values[i] for i in range(held)], at_s)
            got = [lax.ppermute(rel[k], ("core", "z"), route(k)) for k in range(held)]
            return jnp.concatenate(got, 0)

        def tokens_out(values):
            rows = values.astype(LOW).reshape(held, piece, width)
            got = [
                lax.ppermute(rows[k], ("core", "z"), [(d, s) for s, d in route(k)])
                for k in range(held)
            ]
            return jnp.stack(absolute(got, at_s)).astype(F32)

        def gather_tokens(own):
            near = jnp.concatenate(gather_rel(own, "y", n_y), 0)
            return jnp.concatenate([near, swap_core(near)], 0)

        def scatter_dot(left, right, dims):
            half = left.shape[0] // 2
            own = half // n_y
            got = swap_core(mxu(left[half:], right, dims).astype(LOW))

            def sums(r):
                rows = slice(r * own, (r + 1) * own)
                return mxu(left[rows], right, dims) + got[rows].astype(F32)

            arrived = [
                to_offset(sums(r).astype(LOW), "y", r, n_y).astype(F32) for r in range(1, n_y)
            ]
            return sum(arrived, sums(0))

        hidden_own = tokens_in(hidden_in)
        hidden_full = gather_tokens(hidden_own)

        def spread(halves):
            if halves.ndim == 3:
                own = pick(halves, at_c)
                got = swap_core(pick(halves, 1 - at_c))
            else:
                own, got = halves, swap_core(halves)
            both = jnp.where(
                at_c == 0, jnp.concatenate([own, got], 1), jnp.concatenate([got, own], 1)
            )
            over_z = jnp.stack(gather_rel(both, "z", n_z))
            return jnp.concatenate(absolute(gather_rel(over_z, "fx", n_x), at_x), 2)

        def my_heads(blocks):
            if halved:
                return blocks
            by_z = jnp.stack(absolute([blocks[i] for i in range(n_z)], at_z))
            return lax.dynamic_slice_in_dim(by_z, at_c * z_mine, z_mine, 0)

        def in_halves(values):
            return values.reshape((2, values.shape[0] // 2) + values.shape[1:])

        n_q = 3 * k_heads * head_dim
        n_bias = k_heads + 3 + (-(n_q + k_heads + 3)) % 16
        n_qv, n_f1 = b_qv.shape[1], b_fc1.shape[0]
        n_half = 2 if halved else 1
        qkv_units = w_qkv.reshape(own_d, n_half, k_heads, 3, head_dim).transpose(1, 3, 2, 4, 0)
        rows_d = widen(jnp.stack([widen(b_fc1, own_d), b_proj, b_fc2]), own_d)
        rows_d = jnp.concatenate(
            [rows_d, jnp.zeros((n_bias - k_heads - 3, own_d), rows_d.dtype)], 0
        )
        rows_d = jnp.broadcast_to(rows_d, (n_half,) + rows_d.shape)
        qkv_group = jnp.concatenate(
            [
                qkv_units.reshape(n_half, n_q, own_d),
                widen(b_qv, own_d).reshape(n_half, k_heads, own_d),
                rows_d,
            ],
            1,
        )
        fc1_units = in_halves(w_fc1.T)
        fc2_units = in_halves(w_fc2)
        n_fc = fc1_units.shape[1]
        qkv_all = spread(qkv_group if halved else qkv_group[0])
        proj_all = spread(in_halves(w_proj) if halved else w_proj)
        fc1_all = spread(fc1_units)
        fc2_all = spread(fc2_units)
        qkv_matrix = my_heads(qkv_all[:, :n_q]).reshape(z_mine, 3, k_heads * head_dim, width)
        qkv_matrix = qkv_matrix.transpose(1, 0, 2, 3).reshape(z_mine * n_q, width)
        proj_rows = my_heads(proj_all).reshape(heads * head_dim, width)
        fc1_rows = fc1_all.reshape(n_z * n_fc, width)
        fc2_rows = fc2_all.reshape(n_z * n_fc, width)
        bias_all = qkv_all[:, n_q:].astype(F32)
        qv_bias = my_heads(bias_all[:, :k_heads]).reshape(heads, 2 * n_x, own_d)[..., :n_qv]
        qv_bias = qv_bias.reshape(heads, 2 * head_dim)
        span = heads * head_dim
        bias_three = jnp.concatenate(
            [
                qv_bias[:, :head_dim].reshape(1, span),
                jnp.zeros((1, span), F32),
                qv_bias[:, head_dim:].reshape(1, span),
            ],
            1,
        )
        fc1_bias = bias_all[:, k_heads].reshape(n_z, 2, n_x, own_d)[..., :n_f1]
        fc1_bias = pick(fc1_bias, at_c, 1).reshape(1, n_z * n_fc)
        proj_bias = bias_all[0, k_heads + 1 : k_heads + 2]
        fc2_bias = bias_all[0, k_heads + 2 : k_heads + 3]

        cond_act, silu_back = jax.vjp(jax.nn.silu, condition)
        cond_low = cond_act.astype(LOW)
        features = cond_low.shape[1]
        cond_pair = jnp.concatenate(absolute([cond_low, swap_core(cond_low)], at_c), 0)
        cond_twice = [
            jnp.concatenate([rows, rows], 0) for rows in gather_rel(cond_pair, "fx", n_x)
        ]
        cond_all = jnp.concatenate(
            [lax.dynamic_slice_in_dim(rows, at_z, n_z, 0) for rows in cond_twice], 0
        )
        cols = w_mod.shape[1]
        counts = (n_x, n_z)
        bias_here = jnp.where((at_z == 0) & (at_y == 0), b_mod.astype(F32), 0.0)
        mod_terms = mxu(cond_all, w_mod, NN) + bias_here
        mod_cols = [None] * n_x
        for ox in range(n_x):
            for oz in range(n_z):
                term = mod_terms[ox * n_z + oz]
                if ox or oz:
                    term = lax.ppermute(term, ("fx", "z"), pair_perm((ox, oz), counts))
                src = (-ox) % n_x
                mod_cols[src] = term if mod_cols[src] is None else mod_cols[src] + term
        mod_mine = jnp.concatenate(mod_cols)
        sums = [mod_mine, None]
        for oc in range(2):
            for oy in range(n_y):
                if oc == 0 and oy == 0:
                    continue
                got = lax.ppermute(mod_mine, ("core", "y"), pair_perm((oc, oy), (2, n_y)))
                sums[oc] = got if sums[oc] is None else sums[oc] + got
        sums = absolute(sums, at_c)
        by_x = absolute(
            [
                jnp.concatenate([part[i * cols : (i + 1) * cols] for part in sums])
                for i in range(n_x)
            ],
            at_x,
        )
        modulation = jnp.concatenate(by_x)
        shift_one, scale_one, gate_one, shift_two, scale_two, gate_two = (
            modulation[i * width : (i + 1) * width].reshape(1, width) for i in range(6)
        )

        resid_in = hidden_own.astype(F32)
        normed_one, inv_one = layer_norm(resid_in)
        attn_in = (
            layer_norm(hidden_full.astype(F32))[0] * (1.0 + scale_one) + shift_one
        ).astype(LOW)
        rows = attn_in.shape[0]
        projected = (mxu(attn_in, qkv_matrix, NT) + bias_three).astype(LOW)
        attended, log_total = attend(projected, head_dim, rows)
        attn_branch = scatter_dot(attended, proj_rows, NN) + proj_bias
        resid_mid = resid_in + gate_one * attn_branch
        normed_two, inv_two = layer_norm(resid_mid)
        mlp_in = gather_tokens((normed_two * (1.0 + scale_two) + shift_two).astype(LOW))
        pre_act = mxu(mlp_in, fc1_rows, NT) + fc1_bias
        act_float, gelu_back = jax.vjp(gelu_tanh, pre_act)
        act_low = act_float.astype(LOW)
        mlp_branch = scatter_dot(act_low, fc2_rows, NN) + fc2_bias
        block_out = tokens_out(resid_mid + gate_two * mlp_branch)

        grad_own = tokens_in(grad_out)
        grad_full = gather_tokens(grad_own)
        cotangent = grad_own.astype(F32)
        grad_gate_two = jnp.sum(cotangent * mlp_branch, 0)
        grad_mlp_out = (gate_two * grad_full.astype(F32)).astype(LOW)
        grad_act = mxu(grad_mlp_out, fc2_rows, NT)
        grad_pre = gelu_back(grad_act)[0].astype(LOW)
        grad_mlp_in = scatter_dot(grad_pre, fc1_rows, NN)
        grad_fc2 = mxu(act_low, grad_mlp_out, TN)
        grad_fc2_bias = jnp.sum(grad_mlp_out.astype(F32), 0)
        grad_fc1 = mxu(grad_pre, mlp_in, TN)
        grad_fc1_bias = jnp.sum(grad_pre.astype(F32), 0)
        grad_scale_two = jnp.sum(grad_mlp_in * normed_two, 0)
        grad_shift_two = jnp.sum(grad_mlp_in, 0)
        grad_mid = cotangent + norm_back(grad_mlp_in * (1.0 + scale_two), normed_two, inv_two)
        grad_gate_one = jnp.sum(grad_mid * attn_branch, 0)
        grad_attn_out = gather_tokens((gate_one * grad_mid).astype(LOW))
        grad_attended = mxu(grad_attn_out, proj_rows, NT).astype(LOW)
        grad_proj = mxu(attended, grad_attn_out, TN)
        grad_proj_bias = jnp.sum(grad_attn_out.astype(F32), 0)
        grad_parts = attend_back(projected, log_total, grad_attended, head_dim, rows)
        grad_flat = jnp.concatenate(grad_parts, 1)
        grad_attn_in = scatter_dot(grad_flat, qkv_matrix, NN)
        grad_qkv = mxu(grad_flat, attn_in, TN)
        bias_sums = [jnp.sum(part.astype(F32), 0) for part in grad_parts]
        grad_scale_one = jnp.sum(grad_attn_in * normed_one, 0)
        grad_shift_one = jnp.sum(grad_attn_in, 0)
        grad_input = tokens_out(
            grad_mid + norm_back(grad_attn_in * (1.0 + scale_one), normed_one, inv_one)
        )

        def all_z(blocks):
            if halved:
                return blocks
            padded = lax.dynamic_update_slice_in_dim(
                jnp.zeros((n_z,) + blocks.shape[1:], F32), blocks, at_c * z_mine, 0
            )
            return jnp.stack(relative([padded[i] for i in range(n_z)], at_z))

        def collect(groups):
            size = width // n_x
            blocks = [
                jnp.concatenate([g[:, :, i * size : (i + 1) * size] for g in groups], 1)
                for i in range(n_x)
            ]
            total = scatter_rel(relative(blocks, at_x), "fx", n_x)
            total = scatter_rel([total[o] for o in range(n_z)], "z", n_z)
            mine, theirs = relative([total[:, :own_d], total[:, own_d:]], at_c)
            return jnp.stack(absolute([mine, swap_core(theirs)], at_c))

        fc_out = collect([grad_fc1.reshape(n_z, n_fc, width), grad_fc2.reshape(n_z, n_fc, width)])
        grad_w_fc1 = fc_out[:, :n_fc].reshape(2 * n_fc, own_d).T
        grad_w_fc2 = fc_out[:, n_fc:].reshape(2 * n_fc, own_d)
        proj_out = collect([all_z(grad_proj.reshape(z_mine, k_heads * head_dim, width))])
        grad_qkv = grad_qkv.reshape(3, z_mine, k_heads * head_dim, width)
        grad_qkv = all_z(grad_qkv.transpose(1, 0, 2, 3).reshape(z_mine, n_q, width))
        qv_rows = jnp.concatenate(
            [bias_sums[0].reshape(heads, head_dim), bias_sums[2].reshape(heads, head_dim)], 1
        ).reshape(z_mine, k_heads, 2 * n_x, n_qv)
        qv_rows = all_z(widen(qv_rows, own_d).reshape(z_mine, k_heads, width))
        f1_rows = widen(grad_fc1_bias.reshape(n_z, n_x, n_f1), own_d).reshape(n_z, 1, -1)
        none = jnp.zeros_like(f1_rows)
        f1_rows = jnp.concatenate(
            [jnp.where(at_c == 0, f1_rows, none), jnp.where(at_c == 0, none, f1_rows)], 2
        )
        d_rows = jnp.stack([grad_proj_bias, grad_fc2_bias])
        d_rows = jnp.concatenate([d_rows, jnp.zeros((n_bias - k_heads - 3, width), F32)], 0)
        d_rows = jnp.broadcast_to(d_rows, (n_z,) + d_rows.shape)
        qkv_out = collect([grad_qkv, qv_rows, f1_rows, d_rows])
        if not halved:
            proj_out = jnp.sum(proj_out, 0, keepdims=True)
            head_out = jnp.sum(qkv_out, 0, keepdims=True)
        else:
            head_out = qkv_out
        grad_w_proj = proj_out.reshape(heads_here * head_dim, own_d)
        grad_w_qkv = head_out[:, :n_q].reshape(n_half, 3, k_heads, head_dim, own_d)
        grad_w_qkv = grad_w_qkv.transpose(4, 0, 2, 1, 3).reshape(own_d, heads_here, three)
        grad_b_qv = head_out[:, n_q : n_q + k_heads, :n_qv].reshape(heads_here, n_qv)
        row = n_q + k_heads
        grad_b_fc1 = jnp.sum(qkv_out[:, row, :n_f1], 0)
        grad_b_proj = qkv_out[0, row + 1]
        grad_b_fc2 = qkv_out[0, row + 2]

        grad_mod = jnp.concatenate(
            [
                grad_shift_one, grad_scale_one, grad_gate_one,
                grad_shift_two, grad_scale_two, grad_gate_two,
            ]
        )
        blocks = [
            [grad_mod[(2 * i + c) * cols : (2 * i + c + 1) * cols] for c in range(2)]
            for i in range(n_x)
        ]
        blocks = relative([jnp.concatenate(b) for b in blocks], at_x)
        blocks = [relative([b[:cols], b[cols:]], at_c) for b in blocks]
        mine = jnp.concatenate([b[0] for b in blocks])
        other = jnp.concatenate([b[1] for b in blocks])
        total = mine
        for oc in range(2):
            for oy in range(n_y):
                if oc == 0 and oy == 0:
                    continue
                total = total + lax.ppermute(
                    other if oc else mine, ("core", "y"), pair_perm((oc, oy), (2, n_y))
                )
        all_rows = [None] * (n_x * n_z)
        for ox in range(n_x):
            row = total[ox * cols : (ox + 1) * cols]
            for oz in range(n_z):
                got = row
                if ox or oz:
                    got = lax.ppermute(row, ("fx", "z"), pair_perm((ox, oz), counts))
                all_rows[((-ox) % n_x) * n_z + (-oz) % n_z] = got
        grad_modulation = jnp.stack(all_rows)
        grad_b_mod = jnp.sum(grad_modulation, 0)
        grad_mod_low = grad_modulation.astype(LOW)
        grad_w_mod = mxu(cond_all, grad_mod_low, TN)
        cond_terms = mxu(grad_mod_low, w_mod, NT)
        by_offset = []
        for ox in range(n_x):
            rows_x = cond_terms[ox * n_z : (ox + 1) * n_z]
            rows_x = lax.dynamic_slice_in_dim(
                jnp.concatenate([rows_x, rows_x], 0), (n_z - at_z) % n_z, n_z, 0
            )
            by_offset.append(relative([rows_x[:held], rows_x[held:]], at_c))
        total = by_offset[0][0]
        for ox in range(n_x):
            for oc in range(2):
                if ox or oc:
                    total = total + lax.ppermute(
                        by_offset[ox][oc], ("fx", "core"), pair_perm((ox, oc), (n_x, 2))
                    )
        grad_cond = silu_back(total)[0]

        return (
            block_out, grad_input, grad_cond, grad_w_mod, grad_b_mod, grad_w_qkv, grad_b_qv,
            grad_w_proj, grad_b_proj, grad_w_fc1, grad_b_fc1, grad_w_fc2, grad_b_fc2,
        )

    return on_device


def solution(mesh):
    n_f, n_t = mesh.shape["fsdp"], mesh.shape["tp"]
    n_z = 4
    n_x, n_y = n_f // 2, n_t // n_z
    fine = Mesh(mesh.devices.reshape(n_x, 2, n_z, n_y), ("fx", "core", "z", "y"))
    f, t = ("fx", "core"), ("z", "y")
    weights = (
        P(t, f), P(f), P(f, t, None), P(t, f), P(t, f), P(f), P(f, t), P(t + f), P(t, f), P(f),
    )
    placed = (P(f, t, None), P(f, t, None), P(f, t)) + weights
    return jax.shard_map(
        make_body(n_x, n_z, n_y), mesh=fine, in_specs=placed, out_specs=placed, check_vma=False
    )
```

```python
import functools

import jax
import jax.numpy as jnp
from jax import lax
from jax.experimental import pallas as pl
from jax.experimental.pallas import tpu as pltpu
from jax.sharding import Mesh
from jax.sharding import PartitionSpec as P


EPSILON = 1e-06
LOW = jnp.bfloat16
F32 = jnp.float32


def layer_norm(values):
    center_mean = jnp.mean(values, -1, keepdims=True)
    centered = values - center_mean
    variance = jnp.mean(centered * centered, -1, keepdims=True)
    inv_std = lax.rsqrt(variance + EPSILON)
    return (centered * inv_std, inv_std)


def norm_back(grad_normed, normed, inv_std):
    return inv_std * (
        grad_normed
        - jnp.mean(grad_normed, -1, keepdims=True)
        - normed * jnp.mean(grad_normed * normed, -1, keepdims=True)
    )


def gelu_tanh(values):
    return jax.nn.gelu(values, approximate=True)


NT = (((1,), (1,)), ((), ()))
TN = (((0,), (0,)), ((), ()))
NN = (((1,), (0,)), ((), ()))


def mxu(left, right, dims):
    return lax.dot_general(left, right, dims, preferred_element_type=F32)


def attend_kernel(head_dim, query_ref, key_ref, value_ref, out_ref, log_ref):
    scale = head_dim ** (-0.5)
    for h in range(query_ref.shape[1] // head_dim):
        cols = slice(h * head_dim, (h + 1) * head_dim)
        scores = mxu(key_ref[:, cols], query_ref[:, cols], NT) * scale
        top = jnp.max(scores, 0, keepdims=True)
        weights = jnp.exp(scores - top)
        total = jnp.sum(weights, 0, keepdims=True)
        log_ref[h : h + 1, :] = top + jnp.log(total)
        probs_low = (weights * (1.0 / total)).astype(LOW)
        out_ref[:, cols] = mxu(value_ref[:, cols], probs_low, TN).T.astype(LOW)


def attend_back_kernel(
    head_dim, query_ref, key_ref, value_ref, log_ref, grad_ref, out_q, out_k, out_v, sum_k, sum_v
):
    scale = head_dim ** (-0.5)
    step = pl.program_id(0)

    @pl.when(step == 0)
    def _():
        sum_k[...] = jnp.zeros(sum_k.shape, F32)
        sum_v[...] = jnp.zeros(sum_v.shape, F32)

    for h in range(query_ref.shape[1] // head_dim):
        cols = slice(h * head_dim, (h + 1) * head_dim)
        query, key = query_ref[:, cols], key_ref[:, cols]
        grad = grad_ref[:, cols]
        scores = mxu(key, query, NT) * scale
        probs = jnp.exp(scores - log_ref[h : h + 1, :])
        grad_probs = mxu(value_ref[:, cols], grad, NT)
        inner = jnp.sum(probs * grad_probs, 0, keepdims=True)
        grad_scores = (probs * (grad_probs - inner)).astype(LOW)
        sum_v[:, cols] += mxu(probs.astype(LOW), grad, NN)
        sum_k[:, cols] += mxu(grad_scores, query, NN)
        out_q[:, cols] = (mxu(key, grad_scores, TN).T * scale).astype(LOW)

    @pl.when(step == pl.num_programs(0) - 1)
    def _():
        out_k[...] = (sum_k[...] * scale).astype(LOW)
        out_v[...] = sum_v[...].astype(LOW)


def attend(projected, head_dim, block):
    rows, span = projected.shape[0], projected.shape[1] // 3
    log_rows = max(8, span // head_dim)
    return pl.pallas_call(
        functools.partial(attend_kernel, head_dim),
        grid=(rows // block,),
        in_specs=[
            pl.BlockSpec((block, span), lambda i: (i, 0)),
            pl.BlockSpec((rows, span), lambda i: (0, 1)),
            pl.BlockSpec((rows, span), lambda i: (0, 2)),
        ],
        out_specs=[
            pl.BlockSpec((block, span), lambda i: (i, 0)),
            pl.BlockSpec((log_rows, block), lambda i: (0, i)),
        ],
        out_shape=[
            jax.ShapeDtypeStruct((rows, span), LOW),
            jax.ShapeDtypeStruct((log_rows, rows), F32),
        ],
        name="attend",
    )(projected, projected, projected)


def attend_back(projected, log_total, grad_attended, head_dim, block):
    rows, span = grad_attended.shape
    log_rows = log_total.shape[0]
    whole = pl.BlockSpec((rows, span), lambda i: (0, 0))
    by_block = pl.BlockSpec((block, span), lambda i: (i, 0))
    return pl.pallas_call(
        functools.partial(attend_back_kernel, head_dim),
        grid=(rows // block,),
        in_specs=[
            by_block,
            pl.BlockSpec((rows, span), lambda i: (0, 1)),
            pl.BlockSpec((rows, span), lambda i: (0, 2)),
            pl.BlockSpec((log_rows, block), lambda i: (0, i)),
            by_block,
        ],
        out_specs=[by_block, whole, whole],
        out_shape=[jax.ShapeDtypeStruct((rows, span), LOW)] * 3,
        scratch_shapes=[pltpu.VMEM((rows, span), F32), pltpu.VMEM((rows, span), F32)],
        name="attend_back",
    )(projected, projected, projected, log_total, grad_attended)


def relative(blocks, place):
    count = len(blocks)
    if count == 2:
        first, second = blocks
        return [jnp.where(place == 0, first, second), jnp.where(place == 0, second, first)]
    stacked = jnp.stack(blocks)
    return [
        lax.dynamic_index_in_dim(stacked, (o + place) % count, 0, keepdims=False)
        for o in range(count)
    ]


def absolute(blocks, place):
    return relative(blocks, (len(blocks) - place) % len(blocks))


def from_offset(values, name, offset, count):
    return lax.ppermute(values, name, [((d + offset) % count, d) for d in range(count)])


def to_offset(values, name, offset, count):
    return lax.ppermute(values, name, [(d, (d + offset) % count) for d in range(count)])


def gather_rel(values, name, count):
    return [values] + [from_offset(values, name, o, count) for o in range(1, count)]


def scatter_rel(blocks, name, count):
    got = [to_offset(blocks[o].astype(LOW), name, o, count) for o in range(1, count)]
    return sum((g.astype(F32) for g in got), blocks[0].astype(F32))


def pair_perm(offsets, counts):
    (o1, o2), (n1, n2) = offsets, counts
    return [
        (a * n2 + b, ((a + o1) % n1) * n2 + (b + o2) % n2) for a in range(n1) for b in range(n2)
    ]


def widen(values, size):
    return jnp.pad(values, [(0, 0)] * (values.ndim - 1) + [(0, size - values.shape[-1])])


def make_body(n_x, n_z, n_y):
    def on_device(
        hidden_in, grad_out, condition, w_mod, b_mod, w_qkv, b_qv, w_proj, b_proj, w_fc1, b_fc1,
        w_fc2, b_fc2,
    ):
        at_x, at_c = lax.axis_index("fx"), lax.axis_index("core")
        at_z, at_y = lax.axis_index("z"), lax.axis_index("y")
        held, piece, width = hidden_in.shape
        assert n_z == 2 * held
        own_d, heads_here, three = w_qkv.shape
        head_dim = three // 3
        halved = heads_here % 2 == 0
        k_heads = heads_here // 2 if halved else heads_here
        z_mine = n_z if halved else n_z // 2
        heads = z_mine * k_heads

        def swap_core(values):
            return lax.ppermute(values, "core", [(0, 1), (1, 0)])

        def pick(values, index, axis=0):
            return lax.dynamic_index_in_dim(values, index, axis, keepdims=False)

        at_s = at_z % held

        def route(step):
            pairs = []
            for core in range(2):
                for z_from in range(n_z):
                    latent = (z_from % held + step) % held
                    pairs.append(
                        (core * n_z + z_from, (z_from // held) * n_z + core * held + latent)
                    )
            return pairs

        def tokens_in(values):
            rel = relative([values[i] for i in range(held)], at_s)
            got = [lax.ppermute(rel[k], ("core", "z"), route(k)) for k in range(held)]
            return jnp.concatenate(got, 0)

        def tokens_out(values):
            rows = values.astype(LOW).reshape(held, piece, width)
            got = [
                lax.ppermute(rows[k], ("core", "z"), [(d, s) for s, d in route(k)])
                for k in range(held)
            ]
            return jnp.stack(absolute(got, at_s)).astype(F32)

        def gather_tokens(own):
            near = jnp.concatenate(gather_rel(own, "y", n_y), 0)
            return jnp.concatenate([near, swap_core(near)], 0)

        def scatter_dot(left, right, dims):
            half = left.shape[0] // 2
            own = half // n_y
            got = swap_core(mxu(left[half:], right, dims).astype(LOW))

            def sums(r):
                rows = slice(r * own, (r + 1) * own)
                return mxu(left[rows], right, dims) + got[rows].astype(F32)

            arrived = [
                to_offset(sums(r).astype(LOW), "y", r, n_y).astype(F32)
                for r in range(1, n_y)
            ]
            return sum(arrived, sums(0))

        hidden_own = tokens_in(hidden_in)
        hidden_full = gather_tokens(hidden_own)

        def spread(halves):
            if halves.ndim == 3:
                own = pick(halves, at_c)
                got = swap_core(pick(halves, 1 - at_c))
            else:
                own, got = halves, swap_core(halves)
            both = jnp.where(
                at_c == 0, jnp.concatenate([own, got], 1), jnp.concatenate([got, own], 1)
            )
            over_z = jnp.stack(gather_rel(both, "z", n_z))
            return jnp.concatenate(absolute(gather_rel(over_z, "fx", n_x), at_x), 2)

        def my_heads(blocks):
            if halved:
                return blocks
            by_z = jnp.stack(absolute([blocks[i] for i in range(n_z)], at_z))
            return lax.dynamic_slice_in_dim(by_z, at_c * z_mine, z_mine, 0)

        def in_halves(values):
            return values.reshape((2, values.shape[0] // 2) + values.shape[1:])

        n_q = 3 * k_heads * head_dim
        n_p = k_heads * head_dim
        n_bias = k_heads + 3 + (-(n_q + k_heads + 3)) % 16
        n_qv, n_f1 = b_qv.shape[1], b_fc1.shape[0]
        n_half = 2 if halved else 1
        qkv_units = w_qkv.reshape(own_d, n_half, k_heads, 3, head_dim).transpose(1, 3, 2, 4, 0)
        rows_d = widen(jnp.stack([widen(b_fc1, own_d), b_proj, b_fc2]), own_d)
        rows_d = jnp.concatenate(
            [rows_d, jnp.zeros((n_bias - k_heads - 3, own_d), rows_d.dtype)], 0
        )
        rows_d = jnp.broadcast_to(rows_d, (n_half,) + rows_d.shape)
        proj_group = jnp.concatenate(
            [
                w_proj.reshape(n_half, n_p, own_d),
                widen(b_qv, own_d).reshape(n_half, k_heads, own_d),
                rows_d,
            ],
            1,
        )
        fc1_units = in_halves(w_fc1.T)
        fc2_units = in_halves(w_fc2)
        n_fc = fc1_units.shape[1]
        qkv_units = qkv_units.reshape(n_half, n_q, own_d)
        proj_all = spread(proj_group if halved else proj_group[0])
        qkv_all = spread(qkv_units if halved else qkv_units[0])
        fc1_all = spread(fc1_units)
        fc2_all = spread(fc2_units)
        qkv_matrix = my_heads(qkv_all).reshape(z_mine, 3, k_heads * head_dim, width)
        qkv_matrix = qkv_matrix.transpose(1, 0, 2, 3).reshape(z_mine * n_q, width)
        proj_rows = my_heads(proj_all[:, :n_p]).reshape(heads * head_dim, width)
        fc1_rows = fc1_all.reshape(n_z * n_fc, width)
        fc2_rows = fc2_all.reshape(n_z * n_fc, width)
        bias_all = proj_all[:, n_p:].astype(F32)
        qv_bias = my_heads(bias_all[:, :k_heads]).reshape(heads, 2 * n_x, own_d)[..., :n_qv]
        qv_bias = qv_bias.reshape(heads, 2 * head_dim)
        span = heads * head_dim
        bias_three = jnp.concatenate(
            [
                qv_bias[:, :head_dim].reshape(1, span),
                jnp.zeros((1, span), F32),
                qv_bias[:, head_dim:].reshape(1, span),
            ],
            1,
        )
        fc1_bias = bias_all[:, k_heads].reshape(n_z, 2, n_x, own_d)[..., :n_f1]
        fc1_bias = pick(fc1_bias, at_c, 1).reshape(1, n_z * n_fc)
        proj_bias = bias_all[0, k_heads + 1 : k_heads + 2]
        fc2_bias = bias_all[0, k_heads + 2 : k_heads + 3]

        cond_act, silu_back = jax.vjp(jax.nn.silu, condition)
        cond_low = cond_act.astype(LOW)
        cond_pair = jnp.concatenate(absolute([cond_low, swap_core(cond_low)], at_c), 0)
        cond_twice = [jnp.concatenate([rows, rows], 0) for rows in gather_rel(cond_pair, "fx", n_x)]
        cond_all = jnp.concatenate(
            [lax.dynamic_slice_in_dim(rows, at_z, n_z, 0) for rows in cond_twice], 0
        )
        cols = w_mod.shape[1]
        bias_here = jnp.where((at_z == 0) & (at_y == 0), b_mod.astype(F32), 0.0)
        mod_terms = mxu(cond_all, w_mod, NN) + bias_here
        by_source = [mod_terms[:n_z]] + [None] * (n_x - 1)
        for o in range(1, n_x):
            rows_x = mod_terms[o * n_z : (o + 1) * n_z]
            by_source[n_x - o] = to_offset(rows_x, "fx", o, n_x)
        by_dest = [
            jnp.concatenate([rows_x[o] for rows_x in by_source]) for o in range(n_z)
        ]
        mod_mine = by_dest[0]
        for o in range(1, n_z):
            mod_mine = mod_mine + to_offset(by_dest[o], "z", o, n_z)
        sums = [mod_mine, None]
        for oc in range(2):
            for oy in range(n_y):
                if oc == 0 and oy == 0:
                    continue
                got = lax.ppermute(mod_mine, ("core", "y"), pair_perm((oc, oy), (2, n_y)))
                sums[oc] = got if sums[oc] is None else sums[oc] + got
        sums = absolute(sums, at_c)
        by_x = absolute(
            [
                jnp.concatenate([part[i * cols : (i + 1) * cols] for part in sums])
                for i in range(n_x)
            ],
            at_x,
        )
        modulation = jnp.concatenate(by_x)
        shift_one, scale_one, gate_one, shift_two, scale_two, gate_two = (
            modulation[i * width : (i + 1) * width].reshape(1, width) for i in range(6)
        )

        resid_in = hidden_own.astype(F32)
        normed_one, inv_one = layer_norm(resid_in)
        attn_in = (
            layer_norm(hidden_full.astype(F32))[0] * (1.0 + scale_one) + shift_one
        ).astype(LOW)
        rows = attn_in.shape[0]
        projected = (mxu(attn_in, qkv_matrix, NT) + bias_three).astype(LOW)
        attended, log_total = attend(projected, head_dim, rows)
        attn_branch = scatter_dot(attended, proj_rows, NN) + proj_bias
        resid_mid = resid_in + gate_one * attn_branch
        normed_two, inv_two = layer_norm(resid_mid)
        mlp_own = (normed_two * (1.0 + scale_two) + shift_two).astype(LOW)
        mlp_in = gather_tokens(mlp_own)
        pre_act = mxu(mlp_in, fc1_rows, NT) + fc1_bias
        act_float, gelu_back = jax.vjp(gelu_tanh, pre_act)
        act_low = act_float.astype(LOW)
        mlp_branch = scatter_dot(act_low, fc2_rows, NN) + fc2_bias
        block_out = tokens_out(resid_mid + gate_two * mlp_branch)

        grad_own = tokens_in(grad_out)
        grad_full = gather_tokens(grad_own)
        cotangent = grad_own.astype(F32)
        grad_gate_two = jnp.sum(cotangent * mlp_branch, 0)
        grad_mlp_out = (gate_two * grad_full.astype(F32)).astype(LOW)
        grad_act = mxu(grad_mlp_out, fc2_rows, NT)
        grad_pre = gelu_back(grad_act)[0].astype(LOW)
        grad_mlp_in = scatter_dot(grad_pre, fc1_rows, NN)
        grad_fc2 = mxu(act_low, grad_mlp_out, TN)
        grad_fc2_bias = jnp.sum(grad_mlp_out.astype(F32), 0)
        grad_fc1 = mxu(grad_pre, mlp_in, TN)
        grad_fc1_bias = jnp.sum(grad_pre.astype(F32), 0)
        grad_scale_two = jnp.sum(grad_mlp_in * normed_two, 0)
        grad_shift_two = jnp.sum(grad_mlp_in, 0)
        grad_mid = cotangent + norm_back(grad_mlp_in * (1.0 + scale_two), normed_two, inv_two)
        grad_gate_one = jnp.sum(grad_mid * attn_branch, 0)
        grad_attn_out = gather_tokens((gate_one * grad_mid).astype(LOW))
        grad_attended = mxu(grad_attn_out, proj_rows, NT).astype(LOW)
        grad_proj = mxu(attended, grad_attn_out, TN)
        grad_proj_bias = jnp.sum(grad_attn_out.astype(F32), 0)
        grad_parts = attend_back(projected, log_total, grad_attended, head_dim, rows)
        grad_flat = jnp.concatenate(grad_parts, 1)
        grad_attn_in = scatter_dot(grad_flat, qkv_matrix, NN)
        grad_qkv = mxu(grad_flat, attn_in, TN)
        bias_sums = [jnp.sum(part.astype(F32), 0) for part in grad_parts]
        grad_scale_one = jnp.sum(grad_attn_in * normed_one, 0)
        grad_shift_one = jnp.sum(grad_attn_in, 0)
        grad_input = tokens_out(
            grad_mid + norm_back(grad_attn_in * (1.0 + scale_one), normed_one, inv_one),
        )

        def all_z(blocks):
            if halved:
                return blocks
            padded = lax.dynamic_update_slice_in_dim(
                jnp.zeros((n_z,) + blocks.shape[1:], F32), blocks, at_c * z_mine, 0
            )
            return jnp.stack(relative([padded[i] for i in range(n_z)], at_z))

        def collect(groups):
            size = width // n_x
            blocks = [
                jnp.concatenate([g[:, :, i * size : (i + 1) * size] for g in groups], 1)
                for i in range(n_x)
            ]
            total = scatter_rel(relative(blocks, at_x), "fx", n_x)
            total = scatter_rel([total[o] for o in range(n_z)], "z", n_z)
            mine, theirs = relative([total[:, :own_d], total[:, own_d:]], at_c)
            return jnp.stack(absolute([mine, swap_core(theirs)], at_c))

        fc2_out = collect([grad_fc2.reshape(n_z, n_fc, width)])
        grad_w_fc2 = fc2_out.reshape(2 * n_fc, own_d)
        fc1_out = collect([grad_fc1.reshape(n_z, n_fc, width)])
        grad_w_fc1 = fc1_out.reshape(2 * n_fc, own_d).T
        proj_out = collect([all_z(grad_proj.reshape(z_mine, k_heads * head_dim, width))])
        grad_qkv = grad_qkv.reshape(3, z_mine, k_heads * head_dim, width)
        grad_qkv = all_z(grad_qkv.transpose(1, 0, 2, 3).reshape(z_mine, n_q, width))
        qv_rows = jnp.concatenate(
            [bias_sums[0].reshape(heads, head_dim), bias_sums[2].reshape(heads, head_dim)], 1
        ).reshape(z_mine, k_heads, 2 * n_x, n_qv)
        qv_rows = all_z(widen(qv_rows, own_d).reshape(z_mine, k_heads, width))
        f1_rows = widen(grad_fc1_bias.reshape(n_z, n_x, n_f1), own_d).reshape(n_z, 1, -1)
        none = jnp.zeros_like(f1_rows)
        f1_rows = jnp.concatenate(
            [jnp.where(at_c == 0, f1_rows, none), jnp.where(at_c == 0, none, f1_rows)], 2
        )
        d_rows = jnp.stack([grad_proj_bias, grad_fc2_bias])
        d_rows = jnp.concatenate([d_rows, jnp.zeros((n_bias - k_heads - 3, width), F32)], 0)
        d_rows = jnp.broadcast_to(d_rows, (n_z,) + d_rows.shape)
        qkv_out = collect([grad_qkv, qv_rows, f1_rows, d_rows])
        if not halved:
            proj_out = jnp.sum(proj_out, 0, keepdims=True)
            head_out = jnp.sum(qkv_out, 0, keepdims=True)
        else:
            head_out = qkv_out
        grad_w_proj = proj_out.reshape(heads_here * head_dim, own_d)
        grad_w_qkv = head_out[:, :n_q].reshape(n_half, 3, k_heads, head_dim, own_d)
        grad_w_qkv = grad_w_qkv.transpose(4, 0, 2, 1, 3).reshape(own_d, heads_here, three)
        grad_b_qv = head_out[:, n_q : n_q + k_heads, :n_qv].reshape(heads_here, n_qv)
        row = n_q + k_heads
        grad_b_fc1 = jnp.sum(qkv_out[:, row, :n_f1], 0)
        grad_b_proj = qkv_out[0, row + 1]
        grad_b_fc2 = qkv_out[0, row + 2]

        grad_mod = jnp.concatenate(
            [
                grad_shift_one, grad_scale_one, grad_gate_one,
                grad_shift_two, grad_scale_two, grad_gate_two,
            ]
        )
        blocks = [
            [grad_mod[(2 * i + c) * cols : (2 * i + c + 1) * cols] for c in range(2)]
            for i in range(n_x)
        ]
        blocks = relative([jnp.concatenate(b) for b in blocks], at_x)
        blocks = [relative([b[:cols], b[cols:]], at_c) for b in blocks]
        mine = jnp.concatenate([b[0] for b in blocks])
        other = jnp.concatenate([b[1] for b in blocks])
        total = mine
        for oc in range(2):
            for oy in range(n_y):
                if oc == 0 and oy == 0:
                    continue
                total = total + lax.ppermute(
                    other if oc else mine, ("core", "y"), pair_perm((oc, oy), (2, n_y))
                )
        over_z = gather_rel(total, "z", n_z)
        all_rows = [None] * n_x
        for o in range(n_x):
            rows_x = jnp.stack([row[o * cols : (o + 1) * cols] for row in over_z])
            all_rows[-o % n_x] = to_offset(rows_x, "fx", o, n_x) if o else rows_x
        grad_modulation = jnp.concatenate(all_rows, 0)
        grad_b_mod = jnp.sum(grad_modulation, 0)
        grad_mod_low = grad_modulation.astype(LOW)
        grad_w_mod = mxu(cond_all, grad_mod_low, TN)
        cond_terms = mxu(grad_mod_low, w_mod, NT)
        by_offset = []
        for ox in range(n_x):
            rows_x = cond_terms[ox * n_z : (ox + 1) * n_z]
            rows_x = lax.dynamic_slice_in_dim(
                jnp.concatenate([rows_x, rows_x], 0), (n_z - at_z) % n_z, n_z, 0
            )
            by_offset.append(relative([rows_x[:held], rows_x[held:]], at_c))
        total = by_offset[0][0]
        for ox in range(n_x):
            for oc in range(2):
                if ox or oc:
                    total = total + lax.ppermute(
                        by_offset[ox][oc], ("fx", "core"), pair_perm((ox, oc), (n_x, 2))
                    )
        grad_cond = silu_back(total)[0]

        return (
            block_out, grad_input, grad_cond, grad_w_mod, grad_b_mod, grad_w_qkv, grad_b_qv,
            grad_w_proj, grad_b_proj, grad_w_fc1, grad_b_fc1, grad_w_fc2, grad_b_fc2,
        )

    return on_device


def solution(mesh):
    n_f, n_t = mesh.shape["fsdp"], mesh.shape["tp"]
    n_z = 4
    n_x, n_y = n_f // 2, n_t // n_z
    fine = Mesh(mesh.devices.reshape(n_x, 2, n_z, n_y), ("fx", "core", "z", "y"))
    f, t = ("fx", "core"), ("z", "y")
    weights = (
        P(t, f), P(f), P(f, t, None), P(t, f), P(t, f), P(f), P(f, t), P(t + f), P(t, f), P(f),
    )
    placed = (P(f, t, None), P(f, t, None), P(f, t)) + weights
    body = make_body(n_x, n_z, n_y)

    return jax.shard_map(body, mesh=fine, in_specs=placed, out_specs=placed, check_vma=False)
```
